32 devices in a mesh: layer: 16 (over z, x, core), dp: 2 (over y).
Axes of the slice: x: 2, y: 2, z: 4, core: 2. Of those that a mesh axis runs over, the one named last changes fastest.
Arguments:
- weights: float32 [32, 1024, 1024], P('layer', 'dp'), may hold values from -6 to 6
- momentum: float32 [32, 1024, 1024], P('layer', 'dp'), may hold values from -3 to 3
- boundary: float32 [16, 512, 1024], P('layer', 'dp'), may hold values from -6 to 6
- adjoint: float32 [16, 512, 1024], P('layer', 'dp'), may hold values from -6 to 6
- target: float32 [512, 1024], P('dp'), may hold values from -6 to 6
Outputs:
- new_weights: float32 [32, 1024, 1024], P('layer', 'dp')
- new_momentum: float32 [32, 1024, 1024], P('layer', 'dp')
- new_boundary: float32 [16, 512, 1024], P('layer', 'dp')
- new_adjoint: float32 [16, 512, 1024], P('layer', 'dp')
The draws below stay inside these ranges and needn't reach their ends.
All inputs are finite; a program needn't handle non-finite values.
Results may differ from the reference program's by a relative error of at most 0.012.
Values may be sent and summed in bfloat16 or wider, within the bound.
A program may use at most 64 MiB of HBM per device.

```python
import math
import jax
import jax.numpy as jnp
from jax import lax

D = 1024
LPD = 2
STEPS = 2
SWEEPS = 2
GROUPS = 16
LAYERS = 32
ROWS = 512


def block_levels(key, shape, shards, smallest, high):
    loudness = 1.0
    for axis_at, blocks in shards:
        draws = jax.random.uniform(jax.random.fold_in(jax.random.fold_in(key, 6), axis_at), (blocks,), jnp.float32, smallest / len(shards), high / len(shards))
        loudness = loudness * jnp.repeat(jnp.exp(draws), shape[axis_at] // blocks).reshape((-1,) + (1,) * (len(shape) - 1 - axis_at))
    return loudness


def noise(key, extent, deviation, bound, split=(), kind=jnp.bfloat16):
    loudness = block_levels(key, extent, split, -0.22, 0.18) if split else 1.0
    values = jax.random.normal(key, extent, jnp.float32) * deviation * loudness
    return jnp.minimum(jnp.maximum(values, -bound), bound).astype(kind)


def setup_inputs(seed: int = 0) -> dict:
    seeds = jax.random.split(jax.random.key(seed), 6)
    weights = noise(seeds[0], (LAYERS, D, D), 1.0, 6.0, ((0, 16), (1, 2)), jnp.float32)
    momentum = noise(seeds[1], (LAYERS, D, D), 0.5, 3.0, ((0, 16), (1, 2)), jnp.float32)
    boundary = noise(seeds[2], (GROUPS, ROWS, D), 1.0, 6.0, ((0, 16), (1, 2)), jnp.float32)
    adjoint = noise(seeds[3], (GROUPS, ROWS, D), 1.0, 6.0, ((0, 16), (1, 2)), jnp.float32)
    target = noise(seeds[4], (ROWS, D), 1.0, 6.0, ((0, 2),), jnp.float32)
    return dict(weights=weights, momentum=momentum, boundary=boundary, adjoint=adjoint, target=target)


step_size = 0.5
momentum_decay = 0.9
learn_rate = 0.05

def forward_all(current, rounded_weights, width_scale):
    inputs_list = []
    slopes_list = []
    for layer_at in range(LPD):
        rounded = current.astype(jnp.bfloat16)
        product = jnp.einsum('grd,gde->gre', rounded.astype(jnp.float32), rounded_weights[:, layer_at].astype(jnp.float32), precision=lax.Precision.HIGHEST)
        squashed = jnp.tanh(product * width_scale)
        current = current + step_size * squashed
        inputs_list.append(rounded)
        slopes_list.append(squashed)
    return (current, inputs_list, slopes_list)

def backward_all(cotangent, rounded_weights, slopes_list, width_scale):
    for layer_at in reversed(range(LPD)):
        slope = slopes_list[layer_at]
        signal = (cotangent * (1.0 - slope * slope)).astype(jnp.bfloat16)
        pulled = jnp.einsum('gre,gde->grd', signal.astype(jnp.float32), rounded_weights[:, layer_at].astype(jnp.float32), precision=lax.Precision.HIGHEST)
        cotangent = cotangent + step_size * width_scale * pulled
    return cotangent

def gradient_all(cotangent, rounded_weights, inputs_list, slopes_list, width_scale, row_scale):
    grads = [None] * LPD
    for layer_at in reversed(range(LPD)):
        slope = slopes_list[layer_at]
        signal = (cotangent * (1.0 - slope * slope)).astype(jnp.bfloat16)
        grads[layer_at] = jnp.einsum('grd,gre->gde', inputs_list[layer_at].astype(jnp.float32), signal.astype(jnp.float32), precision=lax.Precision.HIGHEST) * row_scale
        if layer_at > 0:
            pulled = jnp.einsum('gre,gde->grd', signal.astype(jnp.float32), rounded_weights[:, layer_at].astype(jnp.float32), precision=lax.Precision.HIGHEST)
            cotangent = cotangent + step_size * width_scale * pulled
    return jnp.stack(grads, axis=1).reshape(LAYERS, D, D)

def reference(weights, momentum, boundary, adjoint, target):
    width_scale = 1.0 / math.sqrt(D)
    row_scale = 1.0 / math.sqrt(ROWS)
    current = boundary
    cotangent = adjoint
    for update_at in range(STEPS):
        rounded_weights = weights.astype(jnp.bfloat16).reshape(GROUPS, LPD, D, D)
        for sweep_at in range(SWEEPS):
            finals, inputs_list, slopes_list = forward_all(current, rounded_weights, width_scale)
            current = jnp.concatenate([current[:1], finals[:-1]], axis=0)
        finals, inputs_list, slopes_list = forward_all(current, rounded_weights, width_scale)
        missing = finals[-1] - target
        for sweep_at in range(SWEEPS):
            starts = backward_all(cotangent, rounded_weights, slopes_list, width_scale)
            cotangent = jnp.concatenate([starts[1:], missing[None]], axis=0)
        grads = gradient_all(cotangent, rounded_weights, inputs_list, slopes_list, width_scale, row_scale)
        momentum = momentum_decay * momentum + grads
        weights = weights - learn_rate * momentum
    return (weights, momentum, current, cotangent)
```

```python
import functools
import math

import jax
import jax.numpy as jnp
from jax import lax
from jax.experimental import pallas as pl
from jax.experimental.pallas import tpu as pltpu
from jax.sharding import PartitionSpec as P

STEPS = 2
SWEEPS = 2

step_size = 0.5
momentum_decay = 0.9
learn_rate = 0.05

MESH = pl.DeviceIdType.MESH
f32 = jnp.float32
bf16 = jnp.bfloat16


def kernel(
    groups, shards,
    w_in, m_in, b_in, a_in, t_in,
    w_out, m_out, b_out, a_out,
    wst, mst, wfull, vfull, xcur, acur, tgt, xw, in0, slopes,
    xb, ab, mids, sigs, stage,
    load_sem, store_sem, w_send, w_recv, v_send, v_recv,
    hop_send, hop_recv, ex_send, ex_recv,
):
    layers, own, width = wst.shape
    rows = xcur.shape[0]
    tile = min(256, width)
    tiles = width // tile
    g = lax.axis_index("layer")
    me = lax.axis_index("dp")
    is_first = g == 0
    is_last = g == groups - 1
    not_first = g > 0
    not_last = g < groups - 1
    width_scale = 1.0 / math.sqrt(width)
    row_scale = 1.0 / math.sqrt(rows * shards)

    def peer(d):
        return lax.rem(me + d, shards)

    def source(d):
        return lax.rem(me + shards - d, shards)

    loads = []
    for l in range(layers):
        loads.append(pltpu.make_async_copy(w_in.at[l], wst.at[l], load_sem.at[l]))
    loads.append(pltpu.make_async_copy(b_in.at[0], xcur, load_sem.at[layers]))
    loads.append(pltpu.make_async_copy(m_in, mst, load_sem.at[layers + 1]))
    loads.append(pltpu.make_async_copy(a_in.at[0], acur, load_sem.at[layers + 2]))
    loads.append(pltpu.make_async_copy(t_in, tgt, load_sem.at[layers + 3]))
    for c in loads:
        c.start()

    barrier = pltpu.get_barrier_semaphore()

    @pl.when(not_first)
    def _():
        pl.semaphore_signal(barrier, inc=1, device_id={"layer": g - 1}, device_id_type=MESH)

    @pl.when(not_last)
    def _():
        pl.semaphore_signal(barrier, inc=1, device_id={"layer": g + 1}, device_id_type=MESH)

    for d in range(1, shards):
        pl.semaphore_signal(barrier, inc=1, device_id={"dp": peer(d)}, device_id_type=MESH)

    own_rows = pl.ds(pl.multiple_of(me * own, own), own)

    def block_copy(buf, l, d, sends, recvs, sender):
        region = buf.at[l, pl.ds(pl.multiple_of(sender * own, own), own)]
        return pltpu.make_async_remote_copy(
            src_ref=region, dst_ref=region,
            send_sem=sends.at[l, d - 1], recv_sem=recvs.at[l, d - 1],
            device_id={"dp": peer(d)}, device_id_type=MESH,
        )

    neighbours = not_first.astype(jnp.int32) + not_last.astype(jnp.int32) + (shards - 1)
    for l in range(layers):
        loads[l].wait()
        wfull[l, own_rows, :] = wst[l].astype(bf16)
        if l == 0:
            pl.semaphore_wait(barrier, neighbours)
        for d in range(1, shards):
            block_copy(wfull, l, d, w_send, w_recv, me).start()
    loads[layers + 1].wait()
    for l in range(layers):
        vfull[l, own_rows, :] = (wst[l] - learn_rate * momentum_decay * mst[l]).astype(bf16)
        for d in range(1, shards):
            block_copy(vfull, l, d, v_send, v_recv, me).start()
    for c in loads[layers:layers + 1] + loads[layers + 2:]:
        c.wait()

    def columns(j, n=tile):
        return pl.ds(pl.multiple_of(j * n, n), n)

    def hop(t, way, s, j):
        slot = jnp.where(s == SWEEPS - 1, me, shards)
        into = (xb, ab)[way]
        return pltpu.make_async_remote_copy(
            src_ref=stage.at[way, s, :, columns(j)],
            dst_ref=into.at[t, slot, :, columns(j)],
            send_sem=hop_send.at[t, way, s, j], recv_sem=hop_recv.at[t, way, s, j],
            device_id={"layer": g + 1 if way == 0 else g - 1}, device_id_type=MESH,
        )

    def exchange(t, way, d, sender):
        into = (xb, ab)[way]
        return pltpu.make_async_remote_copy(
            src_ref=into.at[t, sender], dst_ref=into.at[t, sender],
            send_sem=ex_send.at[t, way, d - 1], recv_sem=ex_recv.at[t, way, d - 1],
            device_id={"dp": peer(d)}, device_id_type=MESH,
        )

    def forward(first_x, keep, emit):
        for l in range(layers):
            last = l == layers - 1
            source_ref = in0 if l == 0 else keep.at[l - 1]

            @pl.loop(0, tiles)
            def _(j):
                cols = columns(j)
                product = jnp.dot(source_ref[...], wfull[l, :, cols], preferred_element_type=f32)
                squashed = jnp.tanh(product * width_scale)
                slopes[l, :, cols] = squashed
                before = first_x(cols) if l == 0 else xw[:, cols]
                after = before + step_size * squashed
                if last:
                    if emit is not None:
                        emit(j, cols, after)
                else:
                    xw[:, cols] = after
                    keep[l, :, cols] = after.astype(bf16)

    def backward(first_a, keep, emit):
        for l in reversed(range(layers)):
            start = first_a if l == layers - 1 else (lambda cols: xw[:, cols])

            @pl.loop(0, tiles)
            def _(j):
                cols = columns(j)
                slope = slopes[l, :, cols]
                keep[l, :, cols] = (start(cols) * (1.0 - slope * slope)).astype(bf16)

            if l == 0 and emit is None:
                continue

            @pl.loop(0, tiles)
            def _(j):
                cols = columns(j)
                pulled = lax.dot_general(
                    keep[l], wfull[l, cols, :], (((1,), (1,)), ((), ())),
                    preferred_element_type=f32,
                )
                after = start(cols) + (step_size * width_scale) * pulled
                if l == 0:
                    emit(j, cols, after)
                else:
                    xw[:, cols] = after

    def own_x(cols):
        return xcur[:, cols]

    def own_a(cols):
        return acur[:, cols]

    for t in range(STEPS):
        own_mids = mids.at[me]
        own_sigs = sigs.at[me]
        if t == 0:
            for l in range(layers):
                for d in range(1, shards):
                    block_copy(wfull, l, d, w_send, w_recv, source(d)).wait_recv()

        @pl.when(is_first)
        def _():
            xb[t, me] = xcur[...].astype(bf16)

        @pl.loop(0, SWEEPS)
        def _(s):
            in0[...] = xcur[...].astype(bf16)

            def emit(j, cols, after):
                stage[0, s, :, cols] = after.astype(bf16)

                @pl.when(not_last)
                def _():
                    hop(t, 0, s, j).start()

            forward(own_x, own_mids, emit)

            @pl.when(not_first)
            def _():
                @pl.loop(0, tiles)
                def _(j):
                    hop(t, 0, s, j).wait_recv()

                slot = jnp.where(s == SWEEPS - 1, me, shards)
                xcur[...] = xb[t, slot].astype(f32)

        for d in range(1, shards):
            exchange(t, 0, d, me).start()
        if t == STEPS - 1:
            b_store = pltpu.make_async_copy(xcur, b_out.at[0], store_sem.at[0])
            b_store.start()
        in0[...] = xcur[...].astype(bf16)

        def finals(j, cols, after):
            @pl.when(is_last)
            def _():
                ab[t, me, :, cols] = (after - tgt[:, cols]).astype(bf16)

        forward(own_x, own_mids, finals)

        @pl.loop(0, SWEEPS)
        def _(s):
            def emit(j, cols, after):
                stage[1, s, :, cols] = after.astype(bf16)

                @pl.when(not_first)
                def _():
                    hop(t, 1, s, j).start()

            backward(own_a, own_sigs, emit)

            @pl.when(not_last)
            def _():
                @pl.loop(0, tiles)
                def _(j):
                    hop(t, 1, s, j).wait_recv()

                slot = jnp.where(s == SWEEPS - 1, me, shards)
                acur[...] = ab[t, slot].astype(f32)

            @pl.when(is_last)
            def _():
                acur[...] = ab[t, me].astype(f32)

        for d in range(1, shards):
            exchange(t, 1, d, me).start()
        if t == STEPS - 1:
            a_store = pltpu.make_async_copy(acur, a_out.at[0], store_sem.at[1])
            a_store.start()
        backward(own_a, own_sigs, None)

        @pl.loop(1, shards)
        def _(d):
            s = source(d)
            exchange(t, 0, d, s).wait_recv()
            in0[...] = xb[t, s]
            forward(lambda cols: xb[t, s, :, cols].astype(f32), mids.at[s], None)
            exchange(t, 1, d, s).wait_recv()
            backward(lambda cols: ab[t, s, :, cols].astype(f32), sigs.at[s], None)

        if t == 0:
            for l in range(layers):
                for d in range(1, shards):
                    block_copy(vfull, l, d, v_send, v_recv, source(d)).wait_recv()
                    block_copy(wfull, l, d, w_send, w_recv, me).wait_send()

        part = min(256, own)
        wide = min(512, width)

        def gradient(l, at, j):
            feats = pl.ds(pl.multiple_of(at, part), part)
            if l == 0:
                left = xb[t, 0:shards, :, feats].reshape(shards * rows, part)
            else:
                left = mids[:, l - 1, :, feats].reshape(shards * rows, part)
            right = sigs[:, l, :, columns(j, wide)].reshape(shards * rows, wide)
            return lax.dot_general(
                left, right, (((0,), (0,)), ((), ())), preferred_element_type=f32
            ) * row_scale

        for l in range(layers):
            @pl.loop(0, own // part)
            def _(i):
                @pl.loop(0, width // wide)
                def _(j):
                    cols = columns(j, wide)
                    here = pl.ds(pl.multiple_of(i * part, part), part)
                    at = me * own + i * part
                    moved = momentum_decay * mst[l, here, cols] + gradient(l, at, j)
                    mst[l, here, cols] = moved
                    fresh = wst[l, here, cols] - learn_rate * moved
                    wst[l, here, cols] = fresh
                    if t < STEPS - 1:
                        there = pl.ds(pl.multiple_of(at, part), part)
                        wfull[l, there, cols] = fresh.astype(bf16)

            if t < STEPS - 1:
                @pl.loop(1, shards)
                def _(d):
                    @pl.loop(0, own // part)
                    def _(i):
                        @pl.loop(0, width // wide)
                        def _(j):
                            cols = columns(j, wide)
                            at = source(d) * own + i * part
                            there = pl.ds(pl.multiple_of(at, part), part)
                            fresh = vfull[l, there, cols].astype(f32) - learn_rate * gradient(l, at, j)
                            wfull[l, there, cols] = fresh.astype(bf16)

        if t == STEPS - 1:
            w_store = pltpu.make_async_copy(wst, w_out, store_sem.at[2])
            m_store = pltpu.make_async_copy(mst, m_out, store_sem.at[3])
            w_store.start()
            m_store.start()

        @pl.loop(0, SWEEPS)
        def _(s):
            @pl.loop(0, tiles)
            def _(j):
                @pl.when(not_last)
                def _():
                    hop(t, 0, s, j).wait_send()

                @pl.when(not_first)
                def _():
                    hop(t, 1, s, j).wait_send()

        for d in range(1, shards):
            exchange(t, 0, d, me).wait_send()
            exchange(t, 1, d, me).wait_send()
            if t == 0:
                for l in range(layers):
                    block_copy(vfull, l, d, v_send, v_recv, me).wait_send()

    for c in (b_store, a_store, w_store, m_store):
        c.wait()


def local(groups, shards, weights, momentum, boundary, adjoint, target):
    layers, own, width = weights.shape
    rows = target.shape[0]
    tiles = width // min(256, width)
    others = max(shards - 1, 1)
    dma = pltpu.SemaphoreType.DMA
    anywhere = pl.BlockSpec(memory_space=pl.ANY)
    return pl.pallas_call(
        functools.partial(kernel, groups, shards),
        out_shape=tuple(
            jax.ShapeDtypeStruct(v.shape, f32) for v in (weights, momentum, boundary, adjoint)
        ),
        in_specs=[anywhere] * 5,
        out_specs=(anywhere,) * 4,
        scratch_shapes=[
            pltpu.VMEM((layers, own, width), f32),
            pltpu.VMEM((layers, own, width), f32),
            pltpu.VMEM((layers, width, width), bf16),
            pltpu.VMEM((layers, width, width), bf16),
            pltpu.VMEM((rows, width), f32),
            pltpu.VMEM((rows, width), f32),
            pltpu.VMEM((rows, width), f32),
            pltpu.VMEM((rows, width), f32),
            pltpu.VMEM((rows, width), bf16),
            pltpu.VMEM((layers, rows, width), f32),
            pltpu.VMEM((STEPS, shards + 1, rows, width), bf16),
            pltpu.VMEM((STEPS, shards + 1, rows, width), bf16),
            pltpu.VMEM((shards, max(layers - 1, 1), rows, width), bf16),
            pltpu.VMEM((shards, layers, rows, width), bf16),
            pltpu.VMEM((2, SWEEPS, rows, width), bf16),
            dma((layers + 4,)),
            dma((4,)),
            dma((layers, others)),
            dma((layers, others)),
            dma((layers, others)),
            dma((layers, others)),
            dma((STEPS, 2, SWEEPS, tiles)),
            dma((STEPS, 2, SWEEPS, tiles)),
            dma((STEPS, 2, others)),
            dma((STEPS, 2, others)),
        ],
        compiler_params=pltpu.CompilerParams(
            collective_id=0, has_side_effects=True, vmem_limit_bytes=63 * 1024 * 1024
        ),
    )(weights, momentum, boundary, adjoint, target)


def solution(mesh):
    placed = P("layer", "dp", None)
    return jax.shard_map(
        functools.partial(local, mesh.shape["layer"], mesh.shape["dp"]),
        mesh=mesh,
        in_specs=(placed,) * 4 + (P("dp", None),),
        out_specs=(placed,) * 4,
        check_vma=False,
    )
```

```python
import functools
import math

import jax
import jax.numpy as jnp
from jax import lax
from jax.experimental import pallas as pl
from jax.experimental.pallas import tpu as pltpu
from jax.sharding import PartitionSpec as P

STEPS = 2
SWEEPS = 2

step_size = 0.5
momentum_decay = 0.9
learn_rate = 0.05

MESH = pl.DeviceIdType.MESH
f32 = jnp.float32
bf16 = jnp.bfloat16


def kernel(
    groups, shards,
    w_in, m_in, b_in, a_in, t_in,
    w_out, m_out, b_out, a_out,
    wst, mst, wfull, vfull, xcur, acur, tgt, xw, in0, slopes,
    xb, ab, mids, sigs, stage,
    load_sem, store_sem, w_send, w_recv, v_send, v_recv,
    hop_send, hop_recv, ex_send, ex_recv,
):
    layers, own, width = wst.shape
    rows = xcur.shape[0]
    tile = min(256, width)
    tiles = width // tile
    g = lax.axis_index("layer")
    me = lax.axis_index("dp")
    is_first = g == 0
    is_last = g == groups - 1
    not_first = g > 0
    not_last = g < groups - 1
    width_scale = 1.0 / math.sqrt(width)
    row_scale = 1.0 / math.sqrt(rows * shards)

    def peer(d):
        return lax.rem(me + d, shards)

    def source(d):
        return lax.rem(me + shards - d, shards)

    loads = []
    for l in range(layers):
        loads.append(pltpu.make_async_copy(w_in.at[l], wst.at[l], load_sem.at[l]))
    loads.append(pltpu.make_async_copy(b_in.at[0], xcur, load_sem.at[layers]))
    loads.append(pltpu.make_async_copy(m_in, mst, load_sem.at[layers + 1]))
    loads.append(pltpu.make_async_copy(a_in.at[0], acur, load_sem.at[layers + 2]))
    loads.append(pltpu.make_async_copy(t_in, tgt, load_sem.at[layers + 3]))
    for c in loads:
        c.start()

    barrier = pltpu.get_barrier_semaphore()

    @pl.when(not_first)
    def _():
        pl.semaphore_signal(barrier, inc=1, device_id={"layer": g - 1}, device_id_type=MESH)

    @pl.when(not_last)
    def _():
        pl.semaphore_signal(barrier, inc=1, device_id={"layer": g + 1}, device_id_type=MESH)

    for d in range(1, shards):
        pl.semaphore_signal(barrier, inc=1, device_id={"dp": peer(d)}, device_id_type=MESH)

    own_rows = pl.ds(pl.multiple_of(me * own, own), own)

    def block_copy(buf, l, d, sends, recvs, sender):
        region = buf.at[l, pl.ds(pl.multiple_of(sender * own, own), own)]
        return pltpu.make_async_remote_copy(
            src_ref=region, dst_ref=region,
            send_sem=sends.at[l, d - 1], recv_sem=recvs.at[l, d - 1],
            device_id={"dp": peer(d)}, device_id_type=MESH,
        )

    neighbours = not_first.astype(jnp.int32) + not_last.astype(jnp.int32) + (shards - 1)
    for l in range(layers):
        loads[l].wait()
        wfull[l, own_rows, :] = wst[l].astype(bf16)
        if l == 0:
            pl.semaphore_wait(barrier, neighbours)
        for d in range(1, shards):
            block_copy(wfull, l, d, w_send, w_recv, me).start()
    def send_v(of):
        for l in of:
            for d in range(1, shards):
                block_copy(vfull, l, d, v_send, v_recv, me).start()

    loads[layers + 1].wait()
    for l in range(layers):
        vfull[l, own_rows, :] = (wst[l] - learn_rate * momentum_decay * mst[l]).astype(bf16)
    spare = range(layers // 2, layers)
    send_v(range(layers // 2))
    for c in loads[layers:layers + 1] + loads[layers + 2:]:
        c.wait()

    def columns(j, n=tile):
        return pl.ds(pl.multiple_of(j * n, n), n)

    def hop(t, way, s, j):
        slot = jnp.where(s == SWEEPS - 1, me, shards)
        into = (xb, ab)[way]
        return pltpu.make_async_remote_copy(
            src_ref=stage.at[way, s, :, columns(j)],
            dst_ref=into.at[t, slot, :, columns(j)],
            send_sem=hop_send.at[t, way, s, j], recv_sem=hop_recv.at[t, way, s, j],
            device_id={"layer": g + 1 if way == 0 else g - 1}, device_id_type=MESH,
        )

    def exchange(t, way, d, sender, j):
        into = (xb, ab)[way]
        region = into.at[t, sender, :, columns(j)]
        return pltpu.make_async_remote_copy(
            src_ref=region, dst_ref=region,
            send_sem=ex_send.at[t, way, d - 1, j], recv_sem=ex_recv.at[t, way, d - 1, j],
            device_id={"dp": peer(d)}, device_id_type=MESH,
        )

    def receive(t, way, s, expects):
        @pl.loop(0, tiles)
        def _(j):
            @pl.when(expects)
            def _():
                hop(t, way, s, j).wait_recv()

            @pl.when(s == SWEEPS - 1)
            def _():
                for d in range(1, shards):
                    exchange(t, way, d, me, j).start()

    def arrive(t, way, d, s):
        @pl.loop(0, tiles)
        def _(j):
            exchange(t, way, d, s, j).wait_recv()

    def forward(first_x, keep, emit):
        for l in range(layers):
            last = l == layers - 1
            source_ref = in0 if l == 0 else keep.at[l - 1]

            size = tile if last and emit is not None else width

            @pl.loop(0, width // size, unroll=True)
            def _(j):
                cols = columns(j, size)
                product = jnp.dot(source_ref[...], wfull[l, :, cols], preferred_element_type=f32)
                squashed = jnp.tanh(product * width_scale)
                slopes[l, :, cols] = squashed
                before = first_x(cols) if l == 0 else xw[:, cols]
                after = before + step_size * squashed
                if last:
                    if emit is not None:
                        emit(j, cols, after)
                else:
                    xw[:, cols] = after
                    keep[l, :, cols] = after.astype(bf16)

    def backward(first_a, keep, emit):
        for l in reversed(range(layers)):
            start = first_a if l == layers - 1 else (lambda cols: xw[:, cols])

            every = pl.ds(0, width)
            slope = slopes[l]
            keep[l] = (start(every) * (1.0 - slope * slope)).astype(bf16)

            if l == 0 and emit is None:
                continue

            size = tile if l == 0 else width

            @pl.loop(0, width // size, unroll=True)
            def _(j):
                cols = columns(j, size)
                pulled = lax.dot_general(
                    keep[l], wfull[l, cols, :], (((1,), (1,)), ((), ())),
                    preferred_element_type=f32,
                )
                after = start(cols) + (step_size * width_scale) * pulled
                if l == 0:
                    emit(j, cols, after)
                else:
                    xw[:, cols] = after

    def own_x(cols):
        return xcur[:, cols]

    def own_a(cols):
        return acur[:, cols]

    for t in range(STEPS):
        own_mids = mids.at[me]
        own_sigs = sigs.at[me]
        if t == 0:
            for l in range(layers):
                for d in range(1, shards):
                    block_copy(wfull, l, d, w_send, w_recv, source(d)).wait_recv()

        @pl.when(is_first)
        def _():
            xb[t, me] = xcur[...].astype(bf16)

        @pl.loop(0, SWEEPS)
        def _(s):
            in0[...] = xcur[...].astype(bf16)

            def emit(j, cols, after):
                stage[0, s, :, cols] = after.astype(bf16)

                @pl.when(not_last)
                def _():
                    hop(t, 0, s, j).start()

            forward(own_x, own_mids, emit)

            receive(t, 0, s, not_first)

            @pl.when(not_first)
            def _():
                slot = jnp.where(s == SWEEPS - 1, me, shards)
                xcur[...] = xb[t, slot].astype(f32)

        if t == STEPS - 1:
            b_store = pltpu.make_async_copy(xcur, b_out.at[0], store_sem.at[0])
            b_store.start()
        in0[...] = xcur[...].astype(bf16)

        def finals(j, cols, after):
            @pl.when(is_last)
            def _():
                ab[t, me, :, cols] = (after - tgt[:, cols]).astype(bf16)

        forward(own_x, own_mids, finals)

        @pl.loop(0, SWEEPS)
        def _(s):
            def emit(j, cols, after):
                stage[1, s, :, cols] = after.astype(bf16)

                @pl.when(not_first)
                def _():
                    hop(t, 1, s, j).start()

            backward(own_a, own_sigs, emit)

            receive(t, 1, s, not_last)

            @pl.when(not_last)
            def _():
                slot = jnp.where(s == SWEEPS - 1, me, shards)
                acur[...] = ab[t, slot].astype(f32)

            @pl.when(is_last)
            def _():
                acur[...] = ab[t, me].astype(f32)

        if t == 0:
            send_v(spare)
        if t == STEPS - 1:
            a_store = pltpu.make_async_copy(acur, a_out.at[0], store_sem.at[1])
            a_store.start()
        backward(own_a, own_sigs, None)

        @pl.loop(1, shards)
        def _(d):
            s = source(d)
            arrive(t, 0, d, s)
            in0[...] = xb[t, s]
            forward(lambda cols: xb[t, s, :, cols].astype(f32), mids.at[s], None)
            arrive(t, 1, d, s)
            backward(lambda cols: ab[t, s, :, cols].astype(f32), sigs.at[s], None)

        if t == 0:
            for l in range(layers):
                for d in range(1, shards):
                    block_copy(wfull, l, d, w_send, w_recv, me).wait_send()

        part = min(512, own)
        wide = width

        def gradient(l, at, j):
            feats = pl.ds(pl.multiple_of(at, part), part)
            if l == 0:
                left = xb[t, 0:shards, :, feats].reshape(shards * rows, part)
            else:
                left = mids[:, l - 1, :, feats].reshape(shards * rows, part)
            right = sigs[:, l, :, columns(j, wide)].reshape(shards * rows, wide)
            return lax.dot_general(
                left, right, (((0,), (0,)), ((), ())), preferred_element_type=f32
            ) * row_scale

        for l in range(layers):
            @pl.loop(0, own // part)
            def _(i):
                @pl.loop(0, width // wide)
                def _(j):
                    cols = columns(j, wide)
                    here = pl.ds(pl.multiple_of(i * part, part), part)
                    at = me * own + i * part
                    moved = momentum_decay * mst[l, here, cols] + gradient(l, at, j)
                    mst[l, here, cols] = moved
                    fresh = wst[l, here, cols] - learn_rate * moved
                    wst[l, here, cols] = fresh
                    if t < STEPS - 1:
                        there = pl.ds(pl.multiple_of(at, part), part)
                        wfull[l, there, cols] = fresh.astype(bf16)

        for l in range(layers if t < STEPS - 1 else 0):
            @pl.loop(1, shards)
            def _(d):
                block_copy(vfull, l, d, v_send, v_recv, source(d)).wait_recv()

                @pl.loop(0, own // part)
                def _(i):
                    @pl.loop(0, width // wide)
                    def _(j):
                        cols = columns(j, wide)
                        at = source(d) * own + i * part
                        there = pl.ds(pl.multiple_of(at, part), part)
                        fresh = vfull[l, there, cols].astype(f32) - learn_rate * gradient(l, at, j)
                        wfull[l, there, cols] = fresh.astype(bf16)

        if t == STEPS - 1:
            w_store = pltpu.make_async_copy(wst, w_out, store_sem.at[2])
            m_store = pltpu.make_async_copy(mst, m_out, store_sem.at[3])
            w_store.start()
            m_store.start()

        @pl.loop(0, SWEEPS)
        def _(s):
            @pl.loop(0, tiles)
            def _(j):
                @pl.when(not_last)
                def _():
                    hop(t, 0, s, j).wait_send()

                @pl.when(not_first)
                def _():
                    hop(t, 1, s, j).wait_send()

        for d in range(1, shards):
            @pl.loop(0, tiles)
            def _(j):
                exchange(t, 0, d, me, j).wait_send()
                exchange(t, 1, d, me, j).wait_send()

            if t == 0:
                for l in range(layers):
                    block_copy(vfull, l, d, v_send, v_recv, me).wait_send()

    for c in (b_store, a_store, w_store, m_store):
        c.wait()


def local(groups, shards, weights, momentum, boundary, adjoint, target):
    layers, own, width = weights.shape
    rows = target.shape[0]
    tiles = width // min(256, width)
    others = max(shards - 1, 1)
    dma = pltpu.SemaphoreType.DMA
    anywhere = pl.BlockSpec(memory_space=pl.ANY)
    return pl.pallas_call(
        functools.partial(kernel, groups, shards),
        out_shape=tuple(
            jax.ShapeDtypeStruct(v.shape, f32) for v in (weights, momentum, boundary, adjoint)
        ),
        in_specs=[anywhere] * 5,
        out_specs=(anywhere,) * 4,
        scratch_shapes=[
            pltpu.VMEM((layers, own, width), f32),
            pltpu.VMEM((layers, own, width), f32),
            pltpu.VMEM((layers, width, width), bf16),
            pltpu.VMEM((layers, width, width), bf16),
            pltpu.VMEM((rows, width), f32),
            pltpu.VMEM((rows, width), f32),
            pltpu.VMEM((rows, width), f32),
            pltpu.VMEM((rows, width), f32),
            pltpu.VMEM((rows, width), bf16),
            pltpu.VMEM((layers, rows, width), f32),
            pltpu.VMEM((STEPS, shards + 1, rows, width), bf16),
            pltpu.VMEM((STEPS, shards + 1, rows, width), bf16),
            pltpu.VMEM((shards, max(layers - 1, 1), rows, width), bf16),
            pltpu.VMEM((shards, layers, rows, width), bf16),
            pltpu.VMEM((2, SWEEPS, rows, width), bf16),
            dma((layers + 4,)),
            dma((4,)),
            dma((layers, others)),
            dma((layers, others)),
            dma((layers, others)),
            dma((layers, others)),
            dma((STEPS, 2, SWEEPS, tiles)),
            dma((STEPS, 2, SWEEPS, tiles)),
            dma((STEPS, 2, others, tiles)),
            dma((STEPS, 2, others, tiles)),
        ],
        compiler_params=pltpu.CompilerParams(
            collective_id=0, has_side_effects=True, vmem_limit_bytes=63 * 1024 * 1024
        ),
    )(weights, momentum, boundary, adjoint, target)


def solution(mesh):
    placed = P("layer", "dp", None)
    return jax.shard_map(
        functools.partial(local, mesh.shape["layer"], mesh.shape["dp"]),
        mesh=mesh,
        in_specs=(placed,) * 4 + (P("dp", None),),
        out_specs=(placed,) * 4,
        check_vma=False,
    )
```
